512 devices in a mesh: rep: 4 (over y), shard: 32 (over z, core), tp: 4 (over x).
Axes of the slice: x: 4, y: 4, z: 16, core: 2. Of those that a mesh axis runs over, the one named last changes fastest.
Arguments:
- qkv_grad: bfloat16 [4, 1024, 3072], P('rep', 'shard', 'tp'), may hold values from -100 to 100
- qkv_error: float32 [4, 1024, 3072], P('rep', 'shard', 'tp'), may hold values from -4 to 4
- qkv_basis: float32 [3072, 32], P('tp'), may hold values from -6 to 6
- qkv_weight: float32 [32, 4, 8, 3072], P('shard', 'rep', None, 'tp'), may hold values from -0.75 to 0.75
- qkv_moment: float32 [32, 4, 8, 3072], P('shard', 'rep', None, 'tp'), may hold values from -0.75 to 0.75
- gu_grad: bfloat16 [4, 1024, 8192], P('rep', 'shard', 'tp'), may hold values from -100 to 100
- gu_error: float32 [4, 1024, 8192], P('rep', 'shard', 'tp'), may hold values from -4 to 4
- gu_basis: float32 [8192, 32], P('tp'), may hold values from -6 to 6
- gu_weight: float32 [32, 4, 8, 8192], P('shard', 'rep', None, 'tp'), may hold values from -0.75 to 0.75
- gu_moment: float32 [32, 4, 8, 8192], P('shard', 'rep', None, 'tp'), may hold values from -0.75 to 0.75
- down_grad: bfloat16 [4, 4096, 1024], P('rep', 'shard', 'tp'), may hold values from -100 to 100
- down_error: float32 [4, 4096, 1024], P('rep', 'shard', 'tp'), may hold values from -4 to 4
- down_basis: float32 [1024, 32], P('tp'), may hold values from -6 to 6
- down_weight: float32 [32, 4, 32, 1024], P('shard', 'rep', None, 'tp'), may hold values from -0.75 to 0.75
- down_moment: float32 [32, 4, 32, 1024], P('shard', 'rep', None, 'tp'), may hold values from -0.75 to 0.75
- vec_grad: bfloat16 [4, 11264], P('rep', ('shard', 'tp')), may hold values from -6 to 6
- vec_weight: float32 [11264], P(('shard', 'tp')), may hold values from 0.5 to 1.5
- vec_moment: float32 [11264], P(('shard', 'tp')), may hold values from -6 to 6
- emb_ids: int32 [4, 4096], P('rep', 'shard'), may hold values from 0 to 31999
- emb_grad: bfloat16 [4, 4096, 1024], P('rep', 'shard', 'tp'), may hold values from -6 to 6
- emb_weight: float32 [32, 4, 250, 1024], P('shard', 'rep', None, 'tp'), may hold values from -0.75 to 0.75
- emb_moment: float32 [32, 4, 250, 1024], P('shard', 'rep', None, 'tp'), may hold values from -6 to 6
Outputs:
- qkv_new: float32 [1024, 3072], P('shard', 'tp')
- qkv_error_new: float32 [4, 1024, 3072], P('rep', 'shard', 'tp')
- qkv_moment_new: float32 [32, 4, 8, 3072], P('shard', 'rep', None, 'tp')
- gu_new: float32 [1024, 8192], P('shard', 'tp')
- gu_error_new: float32 [4, 1024, 8192], P('rep', 'shard', 'tp')
- gu_moment_new: float32 [32, 4, 8, 8192], P('shard', 'rep', None, 'tp')
- down_new: float32 [4096, 1024], P('shard', 'tp')
- down_error_new: float32 [4, 4096, 1024], P('rep', 'shard', 'tp')
- down_moment_new: float32 [32, 4, 32, 1024], P('shard', 'rep', None, 'tp')
- vec_new: float32 [11264], P(('shard', 'tp'))
- vec_moment_new: float32 [11264], P(('shard', 'tp'))
- emb_new: float32 [32000, 1024], P('shard', 'tp')
- emb_moment_new: float32 [32, 4, 250, 1024], P('shard', 'rep', None, 'tp')
The draws below stay inside these ranges and needn't reach their ends.
All inputs are finite; a program needn't handle non-finite values.
Results may differ from the reference program's by a relative error of at most 0.0004.
Values may be sent and summed in bfloat16 or wider, within the bound.
A program may use at most 64 MiB of HBM per device.

```python
import math
import jax
import jax.numpy as jnp
import numpy as np
from jax import lax

D = 1024
FF = 4096
VOCAB = 32000
R = 32
ROUNDS = 2
ROWS = 4096
VEC = 11264
N_REP = 4
N_SHARD = 32


def scaled_grad(key, rows, cols):
    keys = jax.random.split(key, 3)
    position = jnp.arange(rows, dtype=jnp.float32) / (rows - 1)
    row_scale = jnp.exp(position * math.log(3.0) + jax.random.uniform(keys[1], (rows,), jnp.float32, 0.0, math.log(3.3)))
    col_scale = jnp.exp(jax.random.uniform(keys[2], (cols,), jnp.float32, 0.0, math.log(10.0)))
    noise = jax.random.normal(keys[0], (N_REP, rows, cols), jnp.float32)
    values = 0.1 * noise * row_scale[None, :, None] * col_scale[None, None, :]
    return jnp.clip(values, -100.0, 100.0).astype(jnp.bfloat16)


def draw_qkv_grad(key, part):
    return scaled_grad(jax.random.fold_in(key, 11), D, 3 * D)


def draw_gu_grad(key, part):
    return scaled_grad(jax.random.fold_in(key, 12), D, 2 * FF)


def draw_down_grad(key, part):
    return scaled_grad(jax.random.fold_in(key, 13), FF, D)


def set_ends(drawn, own_key, least, high):
    longest = drawn.shape.index(max(drawn.shape))
    spots = []
    for shift in (0, 1):
        where = [jax.random.randint(jax.random.fold_in(own_key, axis), (), 0, length) for axis, length in enumerate(drawn.shape)]
        where[longest] = (where[longest] + shift) % drawn.shape[longest]
        spots.append(tuple(where))
    return drawn.at[spots[0]].set(least).at[spots[1]].set(high)


def shard_levels(stream_key, dims, cuts, low, largest):
    level, own = 1.0, jax.random.fold_in(stream_key, 6)
    for dim, blocks in cuts:
        heights = jnp.exp(jax.random.uniform(jax.random.fold_in(own, dim), (blocks,), jnp.float32, low / len(cuts), largest / len(cuts)))
        level = level * jnp.repeat(heights, dims[dim] // blocks).reshape([-1 if axis == dim else 1 for axis in range(len(dims))])
    return level


def rank_bounds(count, slope):
    portions = [(1 << 20) // math.isqrt(standing ** slope) + 1 for standing in range(1, count + 1)]
    deviation = 1 + sum(portions) // (1 << 30)
    return np.cumsum(np.array([max(1, weight // deviation) for weight in portions]))


def skewed_ids(own_key, shape, number_of, lean):
    listing = rank_bounds(number_of, lean)
    ticket = jax.random.randint(jax.random.fold_in(own_key, 1), shape, 0, int(listing[number_of - 1]))
    standing = jnp.searchsorted(jnp.asarray(listing, jnp.int32), ticket, side="right")
    return jax.random.permutation(jax.random.fold_in(own_key, 2), number_of)[standing].astype(jnp.int32)


def normal_values(own_key, shape, width, limit, cuts=(), kind=jnp.bfloat16):
    values = jax.random.normal(own_key, shape, jnp.float32) * width
    if len(cuts) > 0:
        values = shard_levels(own_key, shape, cuts, -0.22, 0.18) * values
    return jnp.clip(values, min=-limit, max=limit).astype(kind)


def setup_inputs(seed: int = 0) -> dict:
    seeds = jax.random.split(jax.random.key(seed), 23)
    qkv_grad = draw_qkv_grad(jax.random.fold_in(seeds[22], 71), 0)
    qkv_error = normal_values(seeds[1], (N_REP, D, 3 * D), 0.3, 4.0, ((0, 4), (1, 32), (2, 4)), jnp.float32)
    qkv_basis = normal_values(seeds[2], (3 * D, R), 1.0, 6.0, ((0, 4),), jnp.float32)
    qkv_weight = normal_values(seeds[3], (N_SHARD, N_REP, D // (N_SHARD * N_REP), 3 * D), 0.05, 0.75, ((0, 32), (1, 4), (3, 4)), jnp.float32)
    qkv_moment = normal_values(seeds[4], (N_SHARD, N_REP, D // (N_SHARD * N_REP), 3 * D), 0.05, 0.75, ((0, 32), (1, 4), (3, 4)), jnp.float32)
    gu_grad = draw_gu_grad(jax.random.fold_in(seeds[22], 71), 0)
    gu_error = normal_values(seeds[6], (N_REP, D, 2 * FF), 0.3, 4.0, ((0, 4), (1, 32), (2, 4)), jnp.float32)
    gu_basis = normal_values(seeds[7], (2 * FF, R), 1.0, 6.0, ((0, 4),), jnp.float32)
    gu_weight = normal_values(seeds[8], (N_SHARD, N_REP, D // (N_SHARD * N_REP), 2 * FF), 0.05, 0.75, ((0, 32), (1, 4), (3, 4)), jnp.float32)
    gu_moment = normal_values(seeds[9], (N_SHARD, N_REP, D // (N_SHARD * N_REP), 2 * FF), 0.05, 0.75, ((0, 32), (1, 4), (3, 4)), jnp.float32)
    down_grad = draw_down_grad(jax.random.fold_in(seeds[22], 71), 0)
    down_error = normal_values(seeds[11], (N_REP, FF, D), 0.3, 4.0, ((0, 4), (1, 32), (2, 4)), jnp.float32)
    down_basis = normal_values(seeds[12], (D, R), 1.0, 6.0, ((0, 4),), jnp.float32)
    down_weight = normal_values(seeds[13], (N_SHARD, N_REP, FF // (N_SHARD * N_REP), D), 0.05, 0.75, ((0, 32), (1, 4), (3, 4)), jnp.float32)
    down_moment = normal_values(seeds[14], (N_SHARD, N_REP, FF // (N_SHARD * N_REP), D), 0.05, 0.75, ((0, 32), (1, 4), (3, 4)), jnp.float32)
    vec_grad = normal_values(seeds[15], (N_REP, VEC), 1.0, 6.0, ((0, 4), (1, 128)))
    vec_weight = jnp.clip(1.0 + 0.1 * jax.random.normal(seeds[16], (VEC,), jnp.float32), 0.5, 1.5)
    vec_moment = normal_values(seeds[17], (VEC,), 0.5, 6.0, ((0, 128),), jnp.float32)
    emb_ids = set_ends(skewed_ids(seeds[18], (N_REP, ROWS), VOCAB, 2), jax.random.fold_in(seeds[18], 3), 0, VOCAB - 1).astype(jnp.int32)
    emb_grad = normal_values(seeds[19], (N_REP, ROWS, D), 1.0, 6.0, ((0, 4), (1, 32), (2, 4)))
    emb_weight = normal_values(seeds[20], (N_SHARD, N_REP, VOCAB // (N_SHARD * N_REP), D), 0.05, 0.75, ((0, 32), (1, 4), (3, 4)), jnp.float32)
    emb_moment = normal_values(seeds[21], (N_SHARD, N_REP, VOCAB // (N_SHARD * N_REP), D), 0.5, 6.0, ((0, 32), (1, 4), (3, 4)), jnp.float32)
    return {"qkv_grad": qkv_grad, "qkv_error": qkv_error, "qkv_basis": qkv_basis, "qkv_weight": qkv_weight, "qkv_moment": qkv_moment, "gu_grad": gu_grad, "gu_error": gu_error, "gu_basis": gu_basis, "gu_weight": gu_weight, "gu_moment": gu_moment, "down_grad": down_grad, "down_error": down_error, "down_basis": down_basis, "down_weight": down_weight, "down_moment": down_moment, "vec_grad": vec_grad, "vec_weight": vec_weight, "vec_moment": vec_moment, "emb_ids": emb_ids, "emb_grad": emb_grad, "emb_weight": emb_weight, "emb_moment": emb_moment}


momentum_decay = 0.9
step_size = 0.05

def orthonormal(left_factor):
    gram = jnp.dot(left_factor.T, left_factor, precision=lax.Precision.HIGHEST)
    lower_factor = jnp.linalg.cholesky(gram)
    return jax.scipy.linalg.solve_triangular(lower_factor, left_factor.T, lower=True).T

def compress(grad, error, basis):
    full_grad = grad.astype(jnp.float32) + error
    right_factor = basis
    left_factor = None
    for round_index in range(ROUNDS):
        left_factor = jnp.einsum('nio,or->ir', full_grad, right_factor, precision=lax.Precision.HIGHEST)
        left_factor = orthonormal(left_factor)
        right_factor = jnp.einsum('nio,ir->or', full_grad, left_factor, precision=lax.Precision.HIGHEST)
    approx = jnp.dot(left_factor, right_factor.T, precision=lax.Precision.HIGHEST) / N_REP
    return (approx, full_grad - approx[None])

def update(approx, weight, moment):
    moment_new = momentum_decay * moment + approx.reshape(weight.shape)
    weight_new = weight - step_size * moment_new
    return (weight_new.reshape(approx.shape), moment_new)

def reference(qkv_grad, qkv_error, qkv_basis, qkv_weight, qkv_moment, gu_grad, gu_error, gu_basis, gu_weight, gu_moment, down_grad, down_error, down_basis, down_weight, down_moment, vec_grad, vec_weight, vec_moment, emb_ids, emb_grad, emb_weight, emb_moment):
    results = []
    for grad, error, basis, weight, moment in ((qkv_grad, qkv_error, qkv_basis, qkv_weight, qkv_moment), (gu_grad, gu_error, gu_basis, gu_weight, gu_moment), (down_grad, down_error, down_basis, down_weight, down_moment)):
        approx, error_new = compress(grad, error, basis)
        weight_new, moment_new = update(approx, weight, moment)
        results.append((weight_new, error_new, moment_new))
    vec_mean = jnp.sum(vec_grad.astype(jnp.float32), axis=0) / N_REP
    vec_moment_new = momentum_decay * vec_moment + vec_mean
    vec_new = vec_weight - step_size * vec_moment_new
    emb_sum = jax.ops.segment_sum(emb_grad.reshape(-1, D).astype(jnp.float32), emb_ids.reshape(-1).astype(jnp.int32), num_segments=VOCAB) / N_REP
    emb_new, emb_moment_new = update(emb_sum, emb_weight, emb_moment)
    return (results[0][0], results[0][1], results[0][2], results[1][0], results[1][1], results[1][2], results[2][0], results[2][1], results[2][2], vec_new, vec_moment_new, emb_new, emb_moment_new)
```

```python
import jax
import jax.numpy as jnp
from jax import lax
from jax.experimental import pallas as pl
from jax.experimental.pallas import tpu as pltpu
from jax.sharding import PartitionSpec as P

ROUNDS = 2
RANK = 32
GRAM_CHUNK = 24

momentum_decay = 0.9
step_size = 0.05

MESH = pl.DeviceIdType.MESH
HIGH = lax.Precision.HIGHEST


def dot_nn(a, b):
    return lax.dot_general(a, b, (((1,), (0,)), ((), ())), precision=HIGH, preferred_element_type=jnp.float32)


def dot_nt(a, b):
    return lax.dot_general(a, b, (((1,), (1,)), ((), ())), precision=HIGH, preferred_element_type=jnp.float32)


def inverse_factors(grams):
    row = lax.broadcasted_iota(jnp.int32, (RANK, 128), 0)
    lane = lax.broadcasted_iota(jnp.int32, (RANK, 128), 1)
    lefts = list(grams)
    rights = [jnp.where(row == lane, 1.0, 0.0).astype(jnp.float32) for _ in grams]
    for j in range(RANK):
        for m in range(len(lefts)):
            a, e = lefts[m], rights[m]
            pivot = a[j : j + 1, j : j + 1]
            scale = lax.rsqrt(pivot)
            scale = scale * (1.5 - 0.5 * (pivot * scale) * scale)
            row_a = a[j : j + 1, :] * scale
            row_e = e[j : j + 1, :] * scale
            column = a[:, j : j + 1] * scale
            lefts[m] = jnp.where(row > j, a - column * row_a, a)
            rights[m] = jnp.where(row > j, e - column * row_e, jnp.where(row == j, row_e, e))
    return [e[:, :RANK] for e in rights]


def sgd_kernel(rows, cols, *refs):
    (
        qg, qe, qb, gg, ge, gb, dg, de, db, uq, ug, ud, vec,
        approx_q, approx_g, approx_d, gath_q, gath_g, gath_d, vec_sum,
        full_q, full_g, full_d, basis, land_q, land_g, land_d, land_v,
        xbuf, ybuf, wide, half, from_core, from_y, mine, from_z, whole,
        u_send, u_recv, x_send, x_recv, y_send, y_recv, c_send, c_recv,
        ry_send, ry_recv, rz_send, rz_recv, gz_send, gz_recv, gy_send, gy_recv, gc_send, gc_recv,
    ) = refs
    y = lax.axis_index("rep")
    s = lax.axis_index("shard")
    x = lax.axis_index("tp")
    z = s // 2
    core = s % 2
    other = 1 - core

    def at_x(d):
        return (y, s, (x + d) % 4)

    def at_y(d):
        return ((y + d) % 4, s, x)

    def at_z(d):
        return (y, ((z + d) % 16) * 2 + core, x)

    partner = (y, z * 2 + other, x)
    barrier = pltpu.get_barrier_semaphore()
    peers = [at_x(d) for d in (1, 2, 3)] + [at_y(d) for d in (1, 2, 3)]
    peers += [at_z(d) for d in range(1, 16)] + [partner]
    for peer in peers:
        pl.semaphore_signal(barrier, inc=1, device_id=peer, device_id_type=MESH)

    fulls = (full_q, full_g, full_d)
    for full, g, e in zip(fulls, (qg, gg, dg), (qe, ge, de)):
        full[...] = g[0].astype(jnp.float32) + e[0]
    starts = (0, cols[0], cols[0] + cols[1])
    for m, b in enumerate((qb, gb, db)):
        basis[:, starts[m] : starts[m] + cols[m]] = b[...]
    for r in range(ROUNDS):
        xbuf[r, x] = jnp.zeros(xbuf.shape[2:], jnp.float32)
        for c in range(GRAM_CHUNK, 32):
            wide[r, :, c] = jnp.zeros((4, 8, 128), jnp.float32)
    pl.semaphore_wait(barrier, len(peers))

    def copy(src, dst, send, recv, device):
        made = pltpu.make_async_remote_copy(
            src_ref=src, dst_ref=dst, send_sem=send, recv_sem=recv, device_id=device, device_id_type=MESH
        )
        made.start()
        return made

    early = []
    for k, (src, land) in enumerate(((uq, land_q), (ug, land_g), (ud, land_d), (vec, land_v))):
        for d in (1, 2, 3):
            early.append(copy(src, land.at[y], u_send.at[k, d], u_recv.at[k, d], at_y(d)))

    def finish(copies):
        for made in copies:
            made.wait_send()
            made.wait_recv()

    for r in range(ROUNDS):
        for m in range(3):
            part = dot_nt(basis[:, starts[m] : starts[m] + cols[m]], fulls[m][...])
            xbuf[r, x, m, :, : rows[m]] = part
        finish([copy(xbuf.at[r, x], xbuf.at[r, x], x_send.at[r, d], x_recv.at[r, d], at_x(d)) for d in (1, 2, 3)])
        ybuf[r, y] = (xbuf[r, 0] + xbuf[r, 1]) + (xbuf[r, 2] + xbuf[r, 3])
        finish([copy(ybuf.at[r, y], ybuf.at[r, y], y_send.at[r, d], y_recv.at[r, d], at_y(d)) for d in (1, 2, 3)])
        left = (ybuf[r, 0] + ybuf[r, 1]) + (ybuf[r, 2] + ybuf[r, 3])
        for m in range(3):
            raw = dot_nn(left[m][:, : rows[m]], fulls[m][...])
            for c in range(cols[m] // 128):
                wide[r, :, starts[m] // 128 + c] = raw[:, c * 128 : (c + 1) * 128].reshape(4, 8, 128)
            gram = dot_nt(left[m], left[m]) * 0.25
            wide[r, :, GRAM_CHUNK + m, :, :RANK] = gram.reshape(4, 8, RANK)
        finish([copy(wide.at[r, :, pl.ds(other * 16, 16)], from_core.at[r], c_send.at[r], c_recv.at[r], partner)])
        half[r] = wide[r, :, pl.ds(core * 16, 16)] + from_core[r]
        finish([
            copy(half.at[r, (y + d) % 4], from_y.at[r, d - 1], ry_send.at[r, d], ry_recv.at[r, d], at_y(d))
            for d in (1, 2, 3)
        ])
        mine[r] = (half[r, y] + from_y[r, 0]) + (from_y[r, 1] + from_y[r, 2])
        finish([
            copy(mine.at[r, (z + d) % 16], from_z.at[r, d - 1], rz_send.at[r, d], rz_recv.at[r, d], at_z(d))
            for d in range(1, 16)
        ])
        tiles = [mine[r, z]] + [from_z[r, k] for k in range(15)]
        while len(tiles) > 1:
            tiles = [tiles[k] + tiles[k + 1] for k in range(0, len(tiles), 2)]
        whole[r, core, y, z] = tiles[0]
        spot = whole.at[r, core, y, z]
        finish([copy(spot, spot, gz_send.at[r, d], gz_recv.at[r, d], at_z(d)) for d in range(1, 16)])
        spot_y = whole.at[r, core, y]
        finish([copy(spot_y, spot_y, gy_send.at[r, d], gy_recv.at[r, d], at_y(d)) for d in (1, 2, 3)])
        spot_c = whole.at[r, core]
        finish([copy(spot_c, spot_c, gc_send.at[r], gc_recv.at[r], partner)])
        grams = [whole[r, 1, :, GRAM_CHUNK - 16 + m].reshape(RANK, 128) for m in range(3)]
        inverses = inverse_factors(grams)
        for m in range(3):
            first = starts[m] // 128
            chunks = [
                whole[r, c // 16, :, c % 16].reshape(RANK, 128) for c in range(first, first + cols[m] // 128)
            ]
            basis[:, starts[m] : starts[m] + cols[m]] = dot_nn(inverses[m], jnp.concatenate(chunks, axis=1))
    for m, approx in enumerate((approx_q, approx_g, approx_d)):
        ortho = dot_nn(inverses[m], left[m])
        ortho = ortho.T[: rows[m], :]
        approx[...] = dot_nn(ortho, basis[:, starts[m] : starts[m] + cols[m]]) * 0.25
    finish(early)
    for src, land in ((uq, land_q), (ug, land_g), (ud, land_d), (vec, land_v)):
        land[y] = src[...]
    gath_q[...] = land_q[...]
    gath_g[...] = land_g[...]
    gath_d[...] = land_d[...]
    vec_sum[...] = (land_v[0] + land_v[1]) + (land_v[2] + land_v[3])


def power_sgd(grads, errors, bases, updates, vec_tile):
    rows = tuple(g.shape[1] for g in grads)
    cols = tuple(g.shape[2] for g in grads)
    operands = []
    for g, e, b in zip(grads, errors, bases):
        operands += [g, e, b]
    operands += list(updates) + [vec_tile]
    f32 = jnp.float32
    out_shape = [jax.ShapeDtypeStruct((rows[m], cols[m]), f32) for m in range(3)]
    out_shape += [jax.ShapeDtypeStruct((4,) + u.shape, f32) for u in updates]
    out_shape += [jax.ShapeDtypeStruct((8, 128), f32)]
    dma = pltpu.SemaphoreType.DMA
    scratch = [pltpu.VMEM((rows[m], cols[m]), f32) for m in range(3)]
    scratch += [pltpu.VMEM((RANK, sum(cols)), f32)]
    scratch += [pltpu.VMEM((4,) + u.shape, f32) for u in updates]
    scratch += [
        pltpu.VMEM((4, 8, 128), f32),
        pltpu.VMEM((ROUNDS, 4, 3, RANK, 128), f32),
        pltpu.VMEM((ROUNDS, 4, 3, RANK, 128), f32),
        pltpu.VMEM((ROUNDS, 4, 32, 8, 128), f32),
        pltpu.VMEM((ROUNDS, 4, 16, 8, 128), f32),
        pltpu.VMEM((ROUNDS, 4, 16, 8, 128), f32),
        pltpu.VMEM((ROUNDS, 3, 16, 8, 128), f32),
        pltpu.VMEM((ROUNDS, 16, 8, 128), f32),
        pltpu.VMEM((ROUNDS, 15, 8, 128), f32),
        pltpu.VMEM((ROUNDS, 2, 4, 16, 8, 128), f32),
    ]
    for shape in ((4, 4), (ROUNDS, 4), (ROUNDS, 4), (ROUNDS,), (ROUNDS, 4), (ROUNDS, 16), (ROUNDS, 16), (ROUNDS, 4), (ROUNDS,)):
        scratch += [dma(shape), dma(shape)]
    vmem = pl.BlockSpec(memory_space=pltpu.VMEM)

    def body(*refs):
        sgd_kernel(rows, cols, *refs)

    return pl.pallas_call(
        body,
        out_shape=out_shape,
        in_specs=[vmem] * len(operands),
        out_specs=[vmem] * len(out_shape),
        scratch_shapes=scratch,
        compiler_params=pltpu.CompilerParams(collective_id=0, has_side_effects=True, vmem_limit_bytes=24 * 1024 * 1024),
        cost_estimate=pl.CostEstimate(flops=400_000_000, bytes_accessed=400_000_000, transcendentals=0),
        name="power_sgd",
    )(*operands)


def add_rows(ids, values, block_rows):
    groups, stacked, _, width = values.shape[0], 8, values.shape[1], values.shape[2]
    per = ids.shape[1]
    padded = (block_rows + 15) // 16 * 16

    def body(ids_ref, values_ref, out_ref):
        @pl.when(pl.program_id(0) == 0)
        def _():
            out_ref[...] = jnp.zeros_like(out_ref)

        spots = lax.broadcasted_iota(jnp.int32, (padded, stacked * per), 0)
        one_hot = jnp.where(spots == ids_ref[0], 1.0, 0.0).astype(jnp.bfloat16)
        block = values_ref[:, :per, :].reshape(stacked * per, width)
        out_ref[...] += jnp.dot(one_hot, block, preferred_element_type=jnp.float32)

    return pl.pallas_call(
        body,
        grid=(groups // stacked,),
        in_specs=[
            pl.BlockSpec((1, 1, stacked * per), lambda k: (k, 0, 0)),
            pl.BlockSpec((stacked, values.shape[1], width), lambda k: (k, 0, 0)),
        ],
        out_specs=pl.BlockSpec((padded, width), lambda k: (0, 0)),
        out_shape=jax.ShapeDtypeStruct((padded, width), jnp.float32),
        name="add_rows",
    )(ids.reshape(groups // stacked, 1, stacked * per), values)[:block_rows]


def on_device(
    qkv_grad, qkv_error, qkv_basis, qkv_weight, qkv_moment,
    gu_grad, gu_error, gu_basis, gu_weight, gu_moment,
    down_grad, down_error, down_basis, down_weight, down_moment,
    vec_grad, vec_weight, vec_moment,
    emb_ids, emb_grad, emb_weight, emb_moment,
):
    rep_count = lax.axis_size("rep")
    rep_index = lax.axis_index("rep")
    shard_index = lax.axis_index("shard")
    low = (emb_ids[0] % 256).astype(jnp.bfloat16)
    top = (emb_ids[0] // 256).astype(jnp.bfloat16)
    per = emb_ids.shape[1]
    extra = jnp.concatenate([low, top]).reshape(1, 2 * per)
    sent = jnp.concatenate([emb_grad[0], extra, jnp.zeros((15, 2 * per), jnp.bfloat16)], axis=0)
    gathered = lax.all_gather(sent, ("rep", "shard"), axis=0, tiled=True)
    gathered = gathered.reshape(-1, sent.shape[0], sent.shape[1])

    weights = (qkv_weight[0, 0], gu_weight[0, 0], down_weight[0, 0])
    moments = (qkv_moment[0, 0], gu_moment[0, 0], down_moment[0, 0])
    updates = [w - (step_size * momentum_decay) * m for w, m in zip(weights, moments)]
    vec_len = vec_weight.shape[0]
    vec_tile = jnp.pad(vec_grad.astype(jnp.float32), ((0, 7), (0, 128 - vec_len)))
    outs = power_sgd(
        (qkv_grad, gu_grad, down_grad),
        (qkv_error, gu_error, down_error),
        (qkv_basis.T, gu_basis.T, down_basis.T),
        updates,
        vec_tile,
    )
    approxes, olds, vec_sum = outs[:3], outs[3:6], outs[6]
    results = []
    for index, (grad, error) in enumerate(((qkv_grad, qkv_error), (gu_grad, gu_error), (down_grad, down_error))):
        approx = approxes[index]
        error_new = (grad[0].astype(jnp.float32) + error[0] - approx)[None]
        local_rows = weights[index].shape[0]
        own_rows = lax.dynamic_slice_in_dim(approx, rep_index * local_rows, local_rows, 0)
        moment_new = (momentum_decay * moments[index] + own_rows)[None, None]
        plain = olds[index].reshape(approx.shape) - step_size * approx
        results += [plain, error_new, moment_new]
    vec_mean = vec_sum[0, :vec_len] / rep_count
    vec_moment_new = momentum_decay * vec_moment + vec_mean
    vec_new = vec_weight - step_size * vec_moment_new

    block_rows = emb_weight.shape[2]
    row_start = (shard_index * rep_count + rep_index) * block_rows
    digits = gathered[:, per, :].astype(jnp.int32)
    row_ids = digits[:, :per] + 256 * digits[:, per:] - row_start
    emb_sum = add_rows(row_ids, gathered, block_rows) / rep_count
    emb_moment_new = momentum_decay * emb_moment[0, 0] + emb_sum
    emb_flat_new = (emb_weight[0, 0] - step_size * emb_moment_new)[None, None]
    emb_whole = lax.all_gather(emb_flat_new, "rep", axis=1, tiled=True)
    emb_new = emb_whole.reshape(emb_whole.shape[1] * emb_whole.shape[2], emb_whole.shape[3])
    return (*results, vec_new, vec_moment_new, emb_new, emb_moment_new[None, None])


def solution(mesh):
    grouped = P("shard", "rep", None, "tp")
    matrix = P("rep", "shard", "tp")
    per_matrix = (matrix, matrix, P("tp", None), grouped, grouped)
    vector = P(("shard", "tp"))
    return jax.shard_map(
        on_device,
        mesh=mesh,
        in_specs=per_matrix * 3
        + (P("rep", ("shard", "tp")), vector, vector, P("rep", "shard"), matrix, grouped, grouped),
        out_specs=(P("shard", "tp"), matrix, grouped) * 3 + (vector, vector, P("shard", "tp"), grouped),
        check_vma=False,
    )
```

```python
import jax
import jax.numpy as jnp
from jax import lax
from jax.experimental import pallas as pl
from jax.experimental.pallas import tpu as pltpu
from jax.sharding import PartitionSpec as P

ROUNDS = 2
RANK = 32
GRAM_CHUNK = 24

momentum_decay = 0.9
step_size = 0.05

MESH = pl.DeviceIdType.MESH
HIGH = lax.Precision.HIGHEST


def dot_nn(a, b):
    return lax.dot_general(a, b, (((1,), (0,)), ((), ())), precision=HIGH, preferred_element_type=jnp.float32)


def dot_nt(a, b):
    return lax.dot_general(a, b, (((1,), (1,)), ((), ())), precision=HIGH, preferred_element_type=jnp.float32)


def inverse_factors(grams):
    row = lax.broadcasted_iota(jnp.int32, (RANK, 128), 0)
    lane = lax.broadcasted_iota(jnp.int32, (RANK, 128), 1)
    lefts = list(grams)
    rights = [jnp.where(row == lane, 1.0, 0.0).astype(jnp.float32) for _ in grams]
    for j in range(RANK):
        for m in range(len(lefts)):
            a, e = lefts[m], rights[m]
            pivot = a[j : j + 1, j : j + 1]
            scale = lax.rsqrt(pivot)
            scale = scale * (1.5 - 0.5 * (pivot * scale) * scale)
            row_a = a[j : j + 1, :] * scale
            row_e = e[j : j + 1, :] * scale
            column = a[:, j : j + 1] * scale
            lefts[m] = jnp.where(row > j, a - column * row_a, a)
            rights[m] = jnp.where(row > j, e - column * row_e, jnp.where(row == j, row_e, e))
    return [e[:, :RANK] for e in rights]


def sgd_kernel(rows, cols, block_rows, *refs):
    (
        qg_hbm, qe_hbm, qb_hbm, qw_hbm, qm_hbm, gg_hbm, ge_hbm, gb_hbm, gw_hbm, gm_hbm,
        dg_hbm, de_hbm, db_hbm, dw_hbm, dm_hbm, rows_hbm, ew_hbm, em_hbm, ids, vec,
        approx_q, approx_g, approx_d, gath_q, gath_g, gath_d, vec_sum, emb_out, emb_moment_out,
        qg, qe, qb, qw, qm, gg, ge, gb, gw, gm, dg, de, db, dw, dm, ew, em,
        full_q, full_g, full_d, basis, land_q, land_g, land_d, land_v,
        xbuf, ybuf, wide, half, from_core, from_y, mine, from_z, whole,
        blocks, id_rows, part_own, part_send, part_land, emb_land,
        l_sem,
        u_send, u_recv, x_send, x_recv, y_send, y_recv, c_send, c_recv,
        ry_send, ry_recv, rz_send, rz_recv, gz_send, gz_recv, gy_send, gy_recv, gc_send, gc_recv,
        er_send, er_recv, el_send, el_recv, ec_send, ec_recv, p_send, p_recv, e_send, e_recv,
    ) = refs
    f32 = jnp.float32
    y = lax.axis_index("rep")
    s = lax.axis_index("shard")
    x = lax.axis_index("tp")
    z = s // 2
    core = s % 2
    other = 1 - core
    per = rows_hbm.shape[1]

    def at_x(d):
        return (y, s, (x + d) % 4)

    def at_y(d):
        return ((y + d) % 4, s, x)

    def at_z(d):
        return (y, ((z + d) % 16) * 2 + core, x)

    def block_at(d):
        return core * 16 + (z + d + 16) % 16

    partner = (y, z * 2 + other, x)
    barrier = pltpu.get_barrier_semaphore()
    peers = [at_x(d) for d in (1, 2, 3)] + [at_y(d) for d in (1, 2, 3)]
    peers += [at_z(d) for d in range(1, 16)] + [partner]
    for peer in peers:
        pl.semaphore_signal(barrier, inc=1, device_id=peer, device_id_type=MESH)

    own_block = blocks.at[core * 16 + z]
    pairs = [(rows_hbm.at[0], own_block.at[pl.ds(0, per)])]
    pairs += list(zip(
        (qg_hbm, qe_hbm, qb_hbm, gg_hbm, ge_hbm, gb_hbm, dg_hbm, de_hbm, db_hbm,
         qw_hbm, qm_hbm, gw_hbm, gm_hbm, dw_hbm, dm_hbm, ew_hbm, em_hbm),
        (qg, qe, qb, gg, ge, gb, dg, de, db, qw, qm, gw, gm, dw, dm, ew, em),
    ))
    local = [pltpu.make_async_copy(src, dst, l_sem.at[k]) for k, (src, dst) in enumerate(pairs)]
    for made in local:
        made.start()
    digits = jnp.broadcast_to(ids[...], (16, per))
    digits = jnp.concatenate([digits & 255, digits >> 8], axis=1).astype(f32).astype(jnp.bfloat16)
    blocks[core * 16 + z, per : per + 16, :] = digits
    for r in range(ROUNDS):
        xbuf[r, x] = jnp.zeros(xbuf.shape[2:], f32)
        for c in range(GRAM_CHUNK, 32):
            wide[r, :, c] = jnp.zeros((4, 8, 128), f32)
    local[0].wait()
    pl.semaphore_wait(barrier, len(peers))

    def copy(src, dst, send, recv, device):
        made = pltpu.make_async_remote_copy(
            src_ref=src, dst_ref=dst, send_sem=send, recv_sem=recv, device_id=device, device_id_type=MESH
        )
        made.start()
        return made

    def finish(copies):
        for made in copies:
            made.wait_send()
            made.wait_recv()

    ring_right, ring_left, swaps = {}, {}, []

    def ring_step(k):
        spot = blocks.at[block_at(1 - k)]
        ring_right[k] = copy(spot, spot, er_send.at[k], er_recv.at[k], at_z(1))
        if k < 8:
            spot = blocks.at[block_at(k - 1)]
            ring_left[k] = copy(spot, spot, el_send.at[k], el_recv.at[k], at_z(15))

    def swap(d):
        spot = blocks.at[block_at(d)]
        swaps.append(copy(spot, spot, ec_send.at[d % 16], ec_recv.at[d % 16], partner))

    def advance(k):
        ring_right[k].wait_recv()
        if k < 8:
            ring_left[k].wait_recv()
            ring_step(k + 1)
            swap(k)
        swap(-k)

    ring_step(1)
    swap(0)

    for made in local[1:]:
        made.wait()
    fulls = (full_q, full_g, full_d)
    for full, g, e in zip(fulls, (qg, gg, dg), (qe, ge, de)):
        full[...] = g[0].astype(f32) + e[0]
    starts = (0, cols[0], cols[0] + cols[1])
    for m, b in enumerate((qb, gb, db)):
        basis[:, starts[m] : starts[m] + cols[m]] = b[...]
    lands = (land_q, land_g, land_d, land_v)
    for land, w, m in zip(lands, (qw, gw, dw), (qm, gm, dm)):
        land[y] = w[0, 0] - (step_size * momentum_decay) * m[0, 0]
    land_v[y] = vec[...]
    early = []

    def send_early():
        for k, land in enumerate(lands):
            for d in (1, 2, 3):
                early.append(copy(land.at[y], land.at[y], u_send.at[k, d], u_recv.at[k, d], at_y(d)))

    def gather_ids():
        finish(swaps)
        for b in range(32):
            pair = blocks[b, per : per + 16, :].astype(f32)[0:1, :]
            id_rows[b // 4, :, (b % 4) * per : (b % 4 + 1) * per] = pair[:, :per] + 256.0 * pair[:, per:]

    def sum_rows(d, target):
        owner = (y + d) % 4
        spots = lax.broadcasted_iota(jnp.int32, (256, 4 * per), 0) + (s * 4 + owner) * block_rows
        spots = spots.astype(f32)

        def group(g, carry):
            one_hot = jnp.where(spots == id_rows[g], 1.0, 0.0).astype(jnp.bfloat16)
            values = blocks[pl.ds(4 * g, 4), :per, :].reshape(4 * per, 2 * per)
            target[...] += jnp.dot(one_hot, values, preferred_element_type=f32)
            return carry

        target[...] = jnp.zeros(target.shape, f32)
        lax.fori_loop(0, 8, group, 0)

    parts, embs = [], []

    def send_parts():
        for d in (1, 2, 3):
            parts.append(copy(part_send.at[d - 1], part_land.at[d - 1], p_send.at[d], p_recv.at[d], at_y(d)))

    def update_rows():
        finish(parts)
        total = (part_own[...] + part_land[0]) + (part_land[1] + part_land[2])
        moment = momentum_decay * em[...] + total[:block_rows] * 0.25
        emb_moment_out[...] = moment
        emb_land[y, :block_rows] = ew[...] - step_size * moment
        emb_land[y, block_rows:] = jnp.zeros((256 - block_rows, 2 * per), f32)
        for d in (1, 2, 3):
            embs.append(copy(emb_land.at[y], emb_land.at[y], e_send.at[d], e_recv.at[d], at_y(d)))

    def first_ids():
        gather_ids()
        sum_rows(1, part_send.at[0])

    def ring_and_early():
        advance(5)
        send_early()

    beside = {(0, k): (lambda k=k: advance(k + 1)) for k in range(8)}
    beside[0, 4] = ring_and_early
    beside[1, 0] = first_ids
    beside[1, 1] = lambda: sum_rows(2, part_send.at[1])
    beside[1, 2] = lambda: sum_rows(3, part_send.at[2])
    beside[1, 3] = lambda: sum_rows(0, part_own)
    beside[1, 4] = send_parts
    beside[1, 6] = update_rows

    def phase(r, k, copies):
        if (r, k) in beside:
            beside[r, k]()
        finish(copies)

    for r in range(ROUNDS):
        for m in range(3):
            part = dot_nt(basis[:, starts[m] : starts[m] + cols[m]], fulls[m][...])
            xbuf[r, x, m, :, : rows[m]] = part
        phase(r, 0, [copy(xbuf.at[r, x], xbuf.at[r, x], x_send.at[r, d], x_recv.at[r, d], at_x(d)) for d in (1, 2, 3)])
        ybuf[r, y] = (xbuf[r, 0] + xbuf[r, 1]) + (xbuf[r, 2] + xbuf[r, 3])
        phase(r, 1, [copy(ybuf.at[r, y], ybuf.at[r, y], y_send.at[r, d], y_recv.at[r, d], at_y(d)) for d in (1, 2, 3)])
        left = (ybuf[r, 0] + ybuf[r, 1]) + (ybuf[r, 2] + ybuf[r, 3])
        for m in range(3):
            raw = dot_nn(left[m][:, : rows[m]], fulls[m][...])
            for c in range(cols[m] // 128):
                wide[r, :, starts[m] // 128 + c] = raw[:, c * 128 : (c + 1) * 128].reshape(4, 8, 128)
            gram = dot_nt(left[m], left[m]) * 0.25
            wide[r, :, GRAM_CHUNK + m, :, :RANK] = gram.reshape(4, 8, RANK)
        phase(r, 2, [copy(wide.at[r, :, pl.ds(other * 16, 16)], from_core.at[r], c_send.at[r], c_recv.at[r], partner)])
        half[r] = wide[r, :, pl.ds(core * 16, 16)] + from_core[r]
        phase(r, 3, [
            copy(half.at[r, (y + d) % 4], from_y.at[r, d - 1], ry_send.at[r, d], ry_recv.at[r, d], at_y(d))
            for d in (1, 2, 3)
        ])
        mine[r] = (half[r, y] + from_y[r, 0]) + (from_y[r, 1] + from_y[r, 2])
        phase(r, 4, [
            copy(mine.at[r, (z + d) % 16], from_z.at[r, d - 1], rz_send.at[r, d], rz_recv.at[r, d], at_z(d))
            for d in range(1, 16)
        ])
        tiles = [mine[r, z]] + [from_z[r, k] for k in range(15)]
        while len(tiles) > 1:
            tiles = [tiles[k] + tiles[k + 1] for k in range(0, len(tiles), 2)]
        whole[r, core, y, z] = tiles[0]
        spot = whole.at[r, core, y, z]
        phase(r, 5, [copy(spot, spot, gz_send.at[r, d], gz_recv.at[r, d], at_z(d)) for d in range(1, 16)])
        spot_y = whole.at[r, core, y]
        phase(r, 6, [copy(spot_y, spot_y, gy_send.at[r, d], gy_recv.at[r, d], at_y(d)) for d in (1, 2, 3)])
        spot_c = whole.at[r, core]
        phase(r, 7, [copy(spot_c, spot_c, gc_send.at[r], gc_recv.at[r], partner)])
        grams = [whole[r, 1, :, GRAM_CHUNK - 16 + m].reshape(RANK, 128) for m in range(3)]
        inverses = inverse_factors(grams)
        for m in range(3):
            first = starts[m] // 128
            chunks = [
                whole[r, c // 16, :, c % 16].reshape(RANK, 128) for c in range(first, first + cols[m] // 128)
            ]
            basis[:, starts[m] : starts[m] + cols[m]] = dot_nn(inverses[m], jnp.concatenate(chunks, axis=1))
    for m, approx in enumerate((approx_q, approx_g, approx_d)):
        ortho = dot_nn(inverses[m], left[m])
        ortho = ortho.T[: rows[m], :]
        approx[...] = dot_nn(ortho, basis[:, starts[m] : starts[m] + cols[m]]) * 0.25
    finish(early)
    gath_q[...] = land_q[...]
    gath_g[...] = land_g[...]
    gath_d[...] = land_d[...]
    vec_sum[...] = (land_v[0] + land_v[1]) + (land_v[2] + land_v[3])
    for made in list(ring_right.values()) + list(ring_left.values()):
        made.wait_send()
    finish(embs)
    for k in range(4):
        emb_out[k] = emb_land[k, :block_rows]


def power_sgd(matrices, emb_grad, emb_weight, emb_moment, emb_ids, vec_tile):
    rows = tuple(matrix[0].shape[1] for matrix in matrices)
    cols = tuple(matrix[0].shape[2] for matrix in matrices)
    block_rows, width = emb_weight.shape
    per = emb_ids.shape[1]
    far = [operand for matrix in matrices for operand in matrix] + [emb_grad, emb_weight, emb_moment]
    f32 = jnp.float32
    shards = [matrix[3].shape[2:] for matrix in matrices]
    out_shape = [jax.ShapeDtypeStruct((rows[m], cols[m]), f32) for m in range(3)]
    out_shape += [jax.ShapeDtypeStruct((4,) + shape, f32) for shape in shards]
    out_shape += [jax.ShapeDtypeStruct((8, 128), f32)]
    out_shape += [jax.ShapeDtypeStruct((4, block_rows, width), f32), jax.ShapeDtypeStruct((block_rows, width), f32)]
    dma = pltpu.SemaphoreType.DMA
    scratch = [pltpu.VMEM(operand.shape, operand.dtype) for matrix in matrices for operand in matrix]
    scratch += [pltpu.VMEM((block_rows, width), f32)] * 2
    scratch += [pltpu.VMEM((rows[m], cols[m]), f32) for m in range(3)]
    scratch += [pltpu.VMEM((RANK, sum(cols)), f32)]
    scratch += [pltpu.VMEM((4,) + shape, f32) for shape in shards]
    scratch += [
        pltpu.VMEM((4, 8, 128), f32),
        pltpu.VMEM((ROUNDS, 4, 3, RANK, 128), f32),
        pltpu.VMEM((ROUNDS, 4, 3, RANK, 128), f32),
        pltpu.VMEM((ROUNDS, 4, 32, 8, 128), f32),
        pltpu.VMEM((ROUNDS, 4, 16, 8, 128), f32),
        pltpu.VMEM((ROUNDS, 4, 16, 8, 128), f32),
        pltpu.VMEM((ROUNDS, 3, 16, 8, 128), f32),
        pltpu.VMEM((ROUNDS, 16, 8, 128), f32),
        pltpu.VMEM((ROUNDS, 15, 8, 128), f32),
        pltpu.VMEM((ROUNDS, 2, 4, 16, 8, 128), f32),
        pltpu.VMEM((32, per + 16, width), jnp.bfloat16),
        pltpu.VMEM((8, 1, 4 * per), f32),
        pltpu.VMEM((256, width), f32),
        pltpu.VMEM((3, 256, width), f32),
        pltpu.VMEM((3, 256, width), f32),
        pltpu.VMEM((4, 256, width), f32),
        dma((18,)),
    ]
    for shape in (
        (4, 4), (ROUNDS, 4), (ROUNDS, 4), (ROUNDS,), (ROUNDS, 4), (ROUNDS, 16), (ROUNDS, 16), (ROUNDS, 4), (ROUNDS,),
        (9,), (9,), (16,), (4,), (4,),
    ):
        scratch += [dma(shape), dma(shape)]
    vmem = pl.BlockSpec(memory_space=pltpu.VMEM)

    def body(*refs):
        sgd_kernel(rows, cols, block_rows, *refs)

    return pl.pallas_call(
        body,
        out_shape=out_shape,
        in_specs=[pl.BlockSpec(memory_space=pl.ANY)] * len(far) + [vmem] * 2,
        out_specs=[vmem] * len(out_shape),
        scratch_shapes=scratch,
        compiler_params=pltpu.CompilerParams(collective_id=0, has_side_effects=True),
        name="power_sgd",
    )(*far, emb_ids, vec_tile)


def on_device(
    qkv_grad, qkv_error, qkv_basis, qkv_weight, qkv_moment,
    gu_grad, gu_error, gu_basis, gu_weight, gu_moment,
    down_grad, down_error, down_basis, down_weight, down_moment,
    vec_grad, vec_weight, vec_moment,
    emb_ids, emb_grad, emb_weight, emb_moment,
):
    rep_count = lax.axis_size("rep")
    rep_index = lax.axis_index("rep")
    moments = (qkv_moment[0, 0], gu_moment[0, 0], down_moment[0, 0])
    vec_len = vec_weight.shape[0]
    vec_tile = jnp.pad(vec_grad.astype(jnp.float32), ((0, 7), (0, 128 - vec_len)))
    outs = power_sgd(
        (
            (qkv_grad, qkv_error, qkv_basis.T, qkv_weight, qkv_moment),
            (gu_grad, gu_error, gu_basis.T, gu_weight, gu_moment),
            (down_grad, down_error, down_basis.T, down_weight, down_moment),
        ),
        emb_grad, emb_weight[0, 0], emb_moment[0, 0], emb_ids, vec_tile,
    )
    approxes, olds, vec_sum, emb_new, emb_moment_new = outs[:3], outs[3:6], outs[6], outs[7], outs[8]
    results = []
    for index, (grad, error) in enumerate(((qkv_grad, qkv_error), (gu_grad, gu_error), (down_grad, down_error))):
        approx = approxes[index]
        error_new = (grad[0].astype(jnp.float32) + error[0] - approx)[None]
        local_rows = moments[index].shape[0]
        own_rows = lax.dynamic_slice_in_dim(approx, rep_index * local_rows, local_rows, 0)
        moment_new = (momentum_decay * moments[index] + own_rows)[None, None]
        plain = olds[index].reshape(approx.shape) - step_size * approx
        results += [plain, error_new, moment_new]
    vec_mean = vec_sum[0, :vec_len] / rep_count
    vec_moment_new = momentum_decay * vec_moment + vec_mean
    vec_new = vec_weight - step_size * vec_moment_new
    emb_new = emb_new.reshape(-1, emb_new.shape[-1])
    return (*results, vec_new, vec_moment_new, emb_new, emb_moment_new[None, None])


def solution(mesh):
    grouped = P("shard", "rep", None, "tp")
    matrix = P("rep", "shard", "tp")
    per_matrix = (matrix, matrix, P("tp", None), grouped, grouped)
    vector = P(("shard", "tp"))
    return jax.shard_map(
        on_device,
        mesh=mesh,
        in_specs=per_matrix * 3
        + (P("rep", ("shard", "tp")), vector, vector, P("rep", "shard"), matrix, grouped, grouped),
        out_specs=(P("shard", "tp"), matrix, grouped) * 3 + (vector, vector, P("shard", "tp"), grouped),
        check_vma=False,
    )
```

```python
import jax
import jax.numpy as jnp
from jax import lax
from jax.experimental import pallas as pl
from jax.experimental.pallas import tpu as pltpu
from jax.sharding import PartitionSpec as P

ROUNDS = 2
RANK = 32
GRAM_CHUNK = 24

momentum_decay = 0.9
step_size = 0.05

MESH = pl.DeviceIdType.MESH
HIGH = lax.Precision.HIGHEST


def dot_nn(a, b):
    return lax.dot_general(a, b, (((1,), (0,)), ((), ())), precision=HIGH, preferred_element_type=jnp.float32)


def dot_nt(a, b):
    return lax.dot_general(a, b, (((1,), (1,)), ((), ())), precision=HIGH, preferred_element_type=jnp.float32)


def inverse_factors(grams):
    row = lax.broadcasted_iota(jnp.int32, (RANK, 128), 0)
    lane = lax.broadcasted_iota(jnp.int32, (RANK, 128), 1)
    lefts = list(grams)
    rights = [jnp.where(row == lane, 1.0, 0.0).astype(jnp.float32) for _ in grams]
    for j in range(RANK):
        for m in range(len(lefts)):
            a, e = lefts[m], rights[m]
            pivot = a[j : j + 1, j : j + 1]
            scale = lax.rsqrt(pivot)
            scale = scale * (1.5 - 0.5 * (pivot * scale) * scale)
            row_a = a[j : j + 1, :] * scale
            row_e = e[j : j + 1, :] * scale
            column = a[:, j : j + 1] * scale
            lefts[m] = jnp.where(row > j, a - column * row_a, a)
            rights[m] = jnp.where(row > j, e - column * row_e, jnp.where(row == j, row_e, e))
    return [e[:, :RANK] for e in rights]


def sgd_kernel(rows, cols, block_rows, *refs):
    (
        qg_hbm, qe_hbm, qb_hbm, qw_hbm, qm_hbm, gg_hbm, ge_hbm, gb_hbm, gw_hbm, gm_hbm,
        dg_hbm, de_hbm, db_hbm, dw_hbm, dm_hbm, rows_hbm, ew_hbm, em_hbm, ids, vec,
        new_q, new_g, new_d, err_q, err_g, err_d, mom_q, mom_g, mom_d, vec_sum, emb_out, emb_moment_out,
        qg, qe, qb, qw, qm, gg, ge, gb, gw, gm, dg, de, db, dw, dm, ew, em,
        full_q, full_g, full_d, basis, land_q, land_g, land_d, land_v,
        xbuf, ybuf, wide, half, from_core, from_y, mine, from_z, whole,
        blocks, id_rows, part_own, part_send, part_mid, part_land, emb_land,
        l_sem,
        u_send, u_recv, x_send, x_recv, y_send, y_recv, c_send, c_recv,
        ry_send, ry_recv, rz_send, rz_recv, gz_send, gz_recv, gy_send, gy_recv, gc_send, gc_recv,
        er_send, er_recv, el_send, el_recv, ec_send, ec_recv, h_send, h_recv, p_send, p_recv, e_send, e_recv, f_send, f_recv,
    ) = refs
    f32 = jnp.float32
    y = lax.axis_index("rep")
    s = lax.axis_index("shard")
    x = lax.axis_index("tp")
    z = s // 2
    core = s % 2
    other = 1 - core
    per = rows_hbm.shape[1]

    def at_x(d):
        return (y, s, (x + d) % 4)

    def at_y(d):
        return ((y + d) % 4, s, x)

    def at_z(d):
        return (y, ((z + d) % 16) * 2 + core, x)

    def block_at(d):
        return core * 16 + (z + d + 16) % 16

    partner = (y, z * 2 + other, x)
    barrier = pltpu.get_barrier_semaphore()
    peers = [at_x(d) for d in (1, 2, 3)] + [at_y(d) for d in (1, 2, 3)]
    peers += [at_z(d) for d in range(1, 16)] + [partner]
    for peer in peers:
        pl.semaphore_signal(barrier, inc=1, device_id=peer, device_id_type=MESH)

    own_block = blocks.at[core * 16 + z]
    pairs = [(rows_hbm.at[0], own_block.at[pl.ds(0, per)])]
    pairs += list(zip(
        (qg_hbm, qe_hbm, qb_hbm, gg_hbm, ge_hbm, gb_hbm, dg_hbm, de_hbm, db_hbm,
         qw_hbm, qm_hbm, gw_hbm, gm_hbm, dw_hbm, dm_hbm, ew_hbm, em_hbm),
        (qg, qe, qb, gg, ge, gb, dg, de, db, qw, qm, gw, gm, dw, dm, ew, em),
    ))
    local = [pltpu.make_async_copy(src, dst, l_sem.at[k]) for k, (src, dst) in enumerate(pairs)]
    for made in local:
        made.start()
    digits = jnp.broadcast_to(ids[...], (16, per))
    digits = jnp.concatenate([digits & 255, digits >> 8], axis=1).astype(f32).astype(jnp.bfloat16)
    blocks[core * 16 + z, per : per + 16, :] = digits
    for r in range(ROUNDS):
        xbuf[r, x] = jnp.zeros(xbuf.shape[2:], f32)
        for c in range(GRAM_CHUNK, 32):
            wide[r, :, c] = jnp.zeros((4, 8, 128), f32)
    def copy(src, dst, send, recv, device):
        made = pltpu.make_async_remote_copy(
            src_ref=src, dst_ref=dst, send_sem=send, recv_sem=recv, device_id=device, device_id_type=MESH
        )
        made.start()
        return made

    def finish(copies):
        for made in copies:
            made.wait_send()
            made.wait_recv()

    ring_right, ring_left, swaps = {}, {}, []

    def ring_step(k):
        spot = blocks.at[block_at(1 - k)]
        ring_right[k] = copy(spot, spot, er_send.at[k], er_recv.at[k], at_z(1))
        if k < 8:
            spot = blocks.at[block_at(k - 1)]
            ring_left[k] = copy(spot, spot, el_send.at[k], el_recv.at[k], at_z(15))

    def swap(d):
        spot = blocks.at[block_at(d)]
        swaps.append(copy(spot, spot, ec_send.at[d % 16], ec_recv.at[d % 16], partner))

    def advance(k):
        ring_right[k].wait_recv()
        if k < 8:
            ring_left[k].wait_recv()
            ring_step(k + 1)
            swap(k)
        swap(-k)

    for made in local:
        made.wait()
    fulls = (full_q, full_g, full_d)
    for full, g, e in zip(fulls, (qg, gg, dg), (qe, ge, de)):
        full[...] = g[0].astype(f32) + e[0]
    starts = (0, cols[0], cols[0] + cols[1])
    spans = ((0, rows[0]), (rows[0], rows[0] + rows[1]), (0, rows[2]))
    for m, b in enumerate((qb, gb, db)):
        basis[:, starts[m] : starts[m] + cols[m]] = b[...]
    lands = (land_q, land_g, land_d, land_v)
    for land, w, m in zip(lands, (qw, gw, dw), (qm, gm, dm)):
        land[y] = w[0, 0] - (step_size * momentum_decay) * m[0, 0]
    land_v[y] = jnp.zeros((8, 128), f32)
    land_v[y, 0:1, : vec.shape[1]] = vec[...].astype(f32)
    early = []

    def send_early():
        for k, land in enumerate(lands):
            for d in (1, 2, 3):
                early.append(copy(land.at[y], land.at[y], u_send.at[k, d], u_recv.at[k, d], at_y(d)))

    def gather_ids():
        finish(swaps)
        for b in range(32):
            pair = blocks[b, per : per + 16, :].astype(f32)[0:1, :]
            id_rows[b // 4, :, (b % 4) * per : (b % 4 + 1) * per] = pair[:, :per] + 256.0 * pair[:, per:]

    def sum_rows(d, target):
        owner = (y + d) % 4
        spots = lax.broadcasted_iota(jnp.int32, (256, 4 * per), 0) + (s * 4 + owner) * block_rows
        spots = spots.astype(f32)

        def group(g, carry):
            one_hot = jnp.where(spots == id_rows[g], 1.0, 0.0).astype(jnp.bfloat16)
            values = blocks[pl.ds(4 * g, 4), :per, :].reshape(4 * per, 2 * per)
            target[...] += jnp.dot(one_hot, values, preferred_element_type=f32)
            return carry

        target[...] = jnp.zeros(target.shape, f32)
        lax.fori_loop(0, 8, group, 0)

    halves, parts, embs, tails = [], [], [], []

    def send_halves():
        halves.append(copy(part_send.at[1, pl.ds(0, 128)], part_mid.at[0], h_send.at[0], h_recv.at[0], at_y(1)))
        halves.append(copy(part_send.at[1, pl.ds(128, 128)], part_mid.at[1], h_send.at[1], h_recv.at[1], at_y(3)))

    def send_parts():
        finish(halves)
        part_send[0, :128] += part_mid[0]
        part_send[2, 128:] += part_mid[1]
        parts.append(copy(part_send.at[0], part_land.at[0], p_send.at[0], p_recv.at[0], at_y(1)))
        parts.append(copy(part_send.at[2], part_land.at[1], p_send.at[1], p_recv.at[1], at_y(3)))

    def update_rows():
        finish(parts)
        total = part_own[...] + (part_land[0] + part_land[1])
        moment = momentum_decay * em[...].reshape(block_rows, 2 * per) + total[:block_rows] * 0.25
        emb_moment_out[...] = moment
        emb_land[y, :block_rows] = ew[...].reshape(block_rows, 2 * per) - step_size * moment
        emb_land[y, block_rows:] = jnp.zeros((256 - block_rows, 2 * per), f32)
        embs.append(copy(emb_land.at[y], emb_land.at[y], e_send.at[0], e_recv.at[0], at_y(1)))
        embs.append(copy(emb_land.at[y], emb_land.at[y], e_send.at[1], e_recv.at[1], at_y(3)))

    def forward_rows():
        finish(embs)
        spot = emb_land.at[(y + 3) % 4, pl.ds(0, 128)]
        tails.append(copy(spot, spot, f_send.at[0], f_recv.at[0], at_y(1)))
        spot = emb_land.at[(y + 1) % 4, pl.ds(128, 128)]
        tails.append(copy(spot, spot, f_send.at[1], f_recv.at[1], at_y(3)))

    def first_ids():
        gather_ids()
        sum_rows(2, part_send.at[1])

    def ring_and_early():
        advance(5)
        send_early()

    def third_rows():
        send_halves()
        sum_rows(3, part_send.at[2])

    beside = {(0, k): (lambda k=k: advance(k + 1)) for k in range(8)}
    beside[0, 4] = ring_and_early
    beside[1, 0] = first_ids
    beside[1, 1] = lambda: sum_rows(1, part_send.at[0])
    beside[1, 2] = third_rows
    beside[1, 3] = lambda: sum_rows(0, part_own)
    beside[1, 4] = send_parts
    beside[1, 5] = update_rows
    beside[1, 6] = forward_rows

    def phase(r, k, copies):
        if (r, k) in beside:
            beside[r, k]()
        finish(copies)

    for r in range(ROUNDS):
        for m in range(3):
            part = dot_nt(basis[:, starts[m] : starts[m] + cols[m]], fulls[m][...])
            xbuf[r, x, m // 2, :, spans[m][0] : spans[m][1]] = part
        if r == 0:
            pl.semaphore_wait(barrier, len(peers))
            ring_step(1)
            swap(0)
        phase(r, 0, [copy(xbuf.at[r, x], xbuf.at[r, x], x_send.at[r, d], x_recv.at[r, d], at_x(d)) for d in (1, 2, 3)])
        ybuf[r, y] = (xbuf[r, 0] + xbuf[r, 1]) + (xbuf[r, 2] + xbuf[r, 3])
        phase(r, 1, [copy(ybuf.at[r, y], ybuf.at[r, y], y_send.at[r, d], y_recv.at[r, d], at_y(d)) for d in (1, 2, 3)])
        both = (ybuf[r, 0] + ybuf[r, 1]) + (ybuf[r, 2] + ybuf[r, 3])
        left = [both[m // 2][:, spans[m][0] : spans[m][1]] for m in range(3)]
        for m in range(3):
            raw = dot_nn(left[m], fulls[m][...])
            for c in range(cols[m] // 128):
                wide[r, :, starts[m] // 128 + c] = raw[:, c * 128 : (c + 1) * 128].reshape(4, 8, 128)
            gram = dot_nt(left[m], left[m]) * 0.25
            wide[r, :, GRAM_CHUNK + m, :, :RANK] = gram.reshape(4, 8, RANK)
        phase(r, 2, [copy(wide.at[r, :, pl.ds(other * 16, 16)], from_core.at[r], c_send.at[r], c_recv.at[r], partner)])
        half[r] = wide[r, :, pl.ds(core * 16, 16)] + from_core[r]
        phase(r, 3, [
            copy(half.at[r, (y + d) % 4], from_y.at[r, d - 1], ry_send.at[r, d], ry_recv.at[r, d], at_y(d))
            for d in (1, 2, 3)
        ])
        mine[r] = (half[r, y] + from_y[r, 0]) + (from_y[r, 1] + from_y[r, 2])
        phase(r, 4, [
            copy(mine.at[r, (z + d) % 16], from_z.at[r, d - 1], rz_send.at[r, d], rz_recv.at[r, d], at_z(d))
            for d in range(1, 16)
        ])
        tiles = [mine[r, z]] + [from_z[r, k] for k in range(15)]
        while len(tiles) > 1:
            tiles = [tiles[k] + tiles[k + 1] for k in range(0, len(tiles), 2)]
        whole[r, core, y, z] = tiles[0]
        spot = whole.at[r, core, y, z]
        phase(r, 5, [copy(spot, spot, gz_send.at[r, d], gz_recv.at[r, d], at_z(d)) for d in range(1, 16)])
        spot_y = whole.at[r, core, y]
        phase(r, 6, [copy(spot_y, spot_y, gy_send.at[r, d], gy_recv.at[r, d], at_y(d)) for d in (1, 2, 3)])
        spot_c = whole.at[r, core]
        phase(r, 7, [copy(spot_c, spot_c, gc_send.at[r], gc_recv.at[r], partner)])
        grams = [whole[r, 1, :, GRAM_CHUNK - 16 + m].reshape(RANK, 128) for m in range(3)]
        inverses = inverse_factors(grams)
        for m in range(3):
            first = starts[m] // 128
            chunks = [
                whole[r, c // 16, :, c % 16].reshape(RANK, 128) for c in range(first, first + cols[m] // 128)
            ]
            basis[:, starts[m] : starts[m] + cols[m]] = dot_nn(inverses[m], jnp.concatenate(chunks, axis=1))
    finish(early)
    outs = ((new_q, err_q, mom_q, qm), (new_g, err_g, mom_g, gm), (new_d, err_d, mom_d, dm))
    for m, (new, err, mom, old) in enumerate(outs):
        ortho = dot_nn(inverses[m], left[m]).T
        approx = dot_nn(ortho, basis[:, starts[m] : starts[m] + cols[m]]) * 0.25
        err[0] = fulls[m][...] - approx
        new[...] = approx
        own = old.shape[2]
        mom[0, 0] = momentum_decay * old[0, 0] + new[pl.ds(pl.multiple_of(y * own, own), own), :]
        new[...] = lands[m][...].reshape(rows[m], cols[m]) - step_size * approx
    vec_sum[...] = (land_v[0] + land_v[1]) + (land_v[2] + land_v[3])
    for made in list(ring_right.values()) + list(ring_left.values()):
        made.wait_send()
    finish(tails)
    for k in range(4):
        emb_out[k * block_rows : (k + 1) * block_rows, :] = emb_land[k, :block_rows]


def power_sgd(matrices, emb_grad, emb_weight, emb_moment, emb_ids, vec_tile):
    rows = tuple(matrix[0].shape[1] for matrix in matrices)
    cols = tuple(matrix[0].shape[2] for matrix in matrices)
    block_rows, _, width = emb_weight.shape
    per = emb_ids.shape[1]
    far = [operand for matrix in matrices for operand in matrix] + [emb_grad, emb_weight, emb_moment]
    f32 = jnp.float32
    shards = [matrix[3].shape[2:] for matrix in matrices]
    out_shape = [jax.ShapeDtypeStruct((rows[m], cols[m]), f32) for m in range(3)]
    out_shape += [jax.ShapeDtypeStruct((1, rows[m], cols[m]), f32) for m in range(3)]
    out_shape += [jax.ShapeDtypeStruct((1, 1) + shape, f32) for shape in shards]
    out_shape += [jax.ShapeDtypeStruct((8, 128), f32)]
    out_shape += [jax.ShapeDtypeStruct((4 * block_rows, width), f32), jax.ShapeDtypeStruct((block_rows, width), f32)]
    dma = pltpu.SemaphoreType.DMA
    scratch = [pltpu.VMEM(operand.shape, operand.dtype) for matrix in matrices for operand in matrix]
    scratch += [pltpu.VMEM((block_rows, 1, width), f32)] * 2
    scratch += [pltpu.VMEM((rows[m], cols[m]), f32) for m in range(3)]
    scratch += [pltpu.VMEM((RANK, sum(cols)), f32)]
    scratch += [pltpu.VMEM((4,) + shape, f32) for shape in shards]
    scratch += [
        pltpu.VMEM((4, 8, 128), f32),
        pltpu.VMEM((ROUNDS, 4, 2, RANK, 128), f32),
        pltpu.VMEM((ROUNDS, 4, 2, RANK, 128), f32),
        pltpu.VMEM((ROUNDS, 4, 32, 8, 128), f32),
        pltpu.VMEM((ROUNDS, 4, 16, 8, 128), f32),
        pltpu.VMEM((ROUNDS, 4, 16, 8, 128), f32),
        pltpu.VMEM((ROUNDS, 3, 16, 8, 128), f32),
        pltpu.VMEM((ROUNDS, 16, 8, 128), f32),
        pltpu.VMEM((ROUNDS, 15, 8, 128), f32),
        pltpu.VMEM((ROUNDS, 2, 4, 16, 8, 128), f32),
        pltpu.VMEM((32, per + 16, width), jnp.bfloat16),
        pltpu.VMEM((8, 1, 4 * per), f32),
        pltpu.VMEM((256, width), f32),
        pltpu.VMEM((3, 256, width), f32),
        pltpu.VMEM((2, 128, width), f32),
        pltpu.VMEM((2, 256, width), f32),
        pltpu.VMEM((4, 256, width), f32),
        dma((18,)),
    ]
    for shape in (
        (4, 4), (ROUNDS, 4), (ROUNDS, 4), (ROUNDS,), (ROUNDS, 4), (ROUNDS, 16), (ROUNDS, 16), (ROUNDS, 4), (ROUNDS,),
        (9,), (9,), (16,), (2,), (2,), (2,), (2,),
    ):
        scratch += [dma(shape), dma(shape)]
    vmem = pl.BlockSpec(memory_space=pltpu.VMEM)

    def body(*refs):
        sgd_kernel(rows, cols, block_rows, *refs)

    return pl.pallas_call(
        body,
        out_shape=out_shape,
        in_specs=[pl.BlockSpec(memory_space=pl.ANY)] * len(far) + [vmem] * 2,
        out_specs=[vmem] * len(out_shape),
        scratch_shapes=scratch,
        compiler_params=pltpu.CompilerParams(collective_id=0, has_side_effects=True),
        name="power_sgd",
    )(*far, emb_ids, vec_tile)


def place(arrays):
    count = len(arrays)

    def body(*refs):
        sources, targets = refs[:count], refs[count : 2 * count]
        held, load, store = refs[2 * count : 3 * count], refs[3 * count], refs[3 * count + 1]
        loads = [pltpu.make_async_copy(sources[k], held[k], load.at[k]) for k in range(count)]
        stores = [pltpu.make_async_copy(held[k], targets[k], store.at[k]) for k in range(count)]
        for made in loads:
            made.start()
        for k in range(count):
            loads[k].wait()
            stores[k].start()
        for made in stores:
            made.wait()

    far = pl.BlockSpec(memory_space=pl.ANY)
    return pl.pallas_call(
        body,
        out_shape=[jax.ShapeDtypeStruct(a.shape, a.dtype) for a in arrays],
        in_specs=[far] * count,
        out_specs=[far] * count,
        scratch_shapes=[pltpu.VMEM(a.shape, a.dtype) for a in arrays] + [pltpu.SemaphoreType.DMA((count,))] * 2,
        name="place",
    )(*arrays)


def on_device(
    qkv_grad, qkv_error, qkv_basis, qkv_weight, qkv_moment,
    gu_grad, gu_error, gu_basis, gu_weight, gu_moment,
    down_grad, down_error, down_basis, down_weight, down_moment,
    vec_grad, vec_weight, vec_moment,
    emb_ids, emb_grad, emb_weight, emb_moment,
):
    rep_count = lax.axis_size("rep")
    vec_len = vec_weight.shape[0]
    block_rows, width = emb_weight.shape[2:]
    outs = power_sgd(
        (
            (qkv_grad, qkv_error, qkv_basis.T, qkv_weight, qkv_moment),
            (gu_grad, gu_error, gu_basis.T, gu_weight, gu_moment),
            (down_grad, down_error, down_basis.T, down_weight, down_moment),
        ),
        emb_grad, emb_weight.reshape(block_rows, 1, width), emb_moment.reshape(block_rows, 1, width), emb_ids, vec_grad,
    )
    vec_sum, emb_moment_new = outs[9], outs[11]
    new_q, new_g, new_d, err_q, err_g, err_d, mom_q, mom_g, mom_d, emb_new = place(list(outs[:9]) + [outs[10]])
    vec_mean = vec_sum[0, :vec_len] / rep_count
    vec_moment_new = momentum_decay * vec_moment + vec_mean
    vec_new = vec_weight - step_size * vec_moment_new
    return (
        new_q, err_q, mom_q, new_g, err_g, mom_g, new_d, err_d, mom_d,
        vec_new, vec_moment_new, emb_new, emb_moment_new[None, None],
    )


def solution(mesh):
    grouped = P("shard", "rep", None, "tp")
    matrix = P("rep", "shard", "tp")
    per_matrix = (matrix, matrix, P("tp", None), grouped, grouped)
    vector = P(("shard", "tp"))
    return jax.shard_map(
        on_device,
        mesh=mesh,
        in_specs=per_matrix * 3
        + (P("rep", ("shard", "tp")), vector, vector, P("rep", "shard"), matrix, grouped, grouped),
        out_specs=(P("shard", "tp"), matrix, grouped) * 3 + (vector, vector, P("shard", "tp"), grouped),
        check_vma=False,
    )
```

```python
import jax
import jax.numpy as jnp
from jax import lax
from jax.experimental import pallas as pl
from jax.experimental.pallas import tpu as pltpu
from jax.sharding import PartitionSpec as P

ROUNDS = 2
RANK = 32
HALF = 12
USED = 15

momentum_decay = 0.9
step_size = 0.05

MESH = pl.DeviceIdType.MESH
HIGH = lax.Precision.HIGHEST


def dot_nn(a, b):
    return lax.dot_general(a, b, (((1,), (0,)), ((), ())), precision=HIGH, preferred_element_type=jnp.float32)


def dot_nt(a, b):
    return lax.dot_general(a, b, (((1,), (1,)), ((), ())), precision=HIGH, preferred_element_type=jnp.float32)


def inverse_factors(grams):
    row = lax.broadcasted_iota(jnp.int32, (RANK, 128), 0)
    lane = lax.broadcasted_iota(jnp.int32, (RANK, 128), 1)
    lefts = list(grams)
    rights = [jnp.where(row == lane, 1.0, 0.0).astype(jnp.float32) for _ in grams]
    for j in range(RANK):
        for m in range(len(lefts)):
            a, e = lefts[m], rights[m]
            pivot = a[j : j + 1, j : j + 1]
            scale = lax.rsqrt(pivot)
            scale = scale * (1.5 - 0.5 * (pivot * scale) * scale)
            row_a = a[j : j + 1, :] * scale
            row_e = e[j : j + 1, :] * scale
            column = a[:, j : j + 1] * scale
            lefts[m] = jnp.where(row > j, a - column * row_a, a)
            rights[m] = jnp.where(row > j, e - column * row_e, jnp.where(row == j, row_e, e))
    return [e[:, :RANK] for e in rights]


def sgd_kernel(rows, cols, block_rows, *refs):
    (
        qg_hbm, qe_hbm, qb_hbm, qw_hbm, qm_hbm, gg_hbm, ge_hbm, gb_hbm, gw_hbm, gm_hbm,
        dg_hbm, de_hbm, db_hbm, dw_hbm, dm_hbm, rows_hbm, ew_hbm, em_hbm, ids, vec,
        new_q, new_g, new_d, err_q, err_g, err_d, mom_q, mom_g, mom_d, vec_sum, emb_out, emb_moment_out,
        qg, qe, qb, qw, qm, gg, ge, gb, gw, gm, dg, de, db, dw, dm, ew, em,
        full_q, full_g, full_d, basis, land_q, land_g, land_d, land_v,
        xbuf, ybuf, wide, half, from_core, from_y, mine, from_z, whole,
        blocks, id_rows, part_own, part_send, part_mid, part_land, emb_land,
        l_sem,
        u_send, u_recv, x_send, x_recv, y_send, y_recv, c_send, c_recv,
        ry_send, ry_recv, rz_send, rz_recv, gz_send, gz_recv, gy_send, gy_recv, gc_send, gc_recv,
        er_send, er_recv, el_send, el_recv, ec_send, ec_recv, h_send, h_recv, p_send, p_recv, e_send, e_recv, f_send, f_recv,
    ) = refs
    f32 = jnp.float32
    y = lax.axis_index("rep")
    s = lax.axis_index("shard")
    x = lax.axis_index("tp")
    z = s // 2
    core = s % 2
    other = 1 - core
    per = rows_hbm.shape[1]

    def at_x(d):
        return (y, s, (x + d) % 4)

    def at_y(d):
        return ((y + d) % 4, s, x)

    def at_z(d):
        return (y, ((z + d) % 16) * 2 + core, x)

    def block_at(d):
        return core * 16 + (z + d + 16) % 16

    partner = (y, z * 2 + other, x)
    barrier = pltpu.get_barrier_semaphore()
    peers = [at_x(d) for d in (1, 2, 3)] + [at_y(d) for d in (1, 2, 3)]
    peers += [at_z(d) for d in range(1, 16)] + [partner]
    for peer in peers:
        pl.semaphore_signal(barrier, inc=1, device_id=peer, device_id_type=MESH)

    own_block = blocks.at[core * 16 + z]
    pairs = [(rows_hbm.at[0], own_block.at[pl.ds(0, per)])]
    pairs += list(zip(
        (qg_hbm, qe_hbm, qb_hbm, gg_hbm, ge_hbm, gb_hbm, dg_hbm, de_hbm, db_hbm,
         qw_hbm, qm_hbm, gw_hbm, gm_hbm, dw_hbm, dm_hbm, ew_hbm, em_hbm),
        (qg, qe, qb, gg, ge, gb, dg, de, db, qw, qm, gw, gm, dw, dm, ew, em),
    ))
    local = [pltpu.make_async_copy(src, dst, l_sem.at[k]) for k, (src, dst) in enumerate(pairs)]
    for made in local:
        made.start()
    digits = jnp.broadcast_to(ids[...], (16, per))
    digits = jnp.concatenate([digits & 255, digits >> 8], axis=1).astype(f32).astype(jnp.bfloat16)
    blocks[core * 16 + z, per : per + 16, :] = digits
    for r in range(ROUNDS):
        xbuf[r, x] = jnp.zeros(xbuf.shape[2:], f32)
        mine[r, USED] = jnp.zeros((8, 128), f32)
        for c in range(HALF, USED):
            wide[r, :, c] = jnp.zeros((4, 8, 128), f32)
            wide[r, :, 16 + c] = jnp.zeros((4, 8, 128), f32)
    def copy(src, dst, send, recv, device):
        made = pltpu.make_async_remote_copy(
            src_ref=src, dst_ref=dst, send_sem=send, recv_sem=recv, device_id=device, device_id_type=MESH
        )
        made.start()
        return made

    def finish(copies):
        for made in copies:
            made.wait_send()
            made.wait_recv()

    ring_right, ring_left, swaps = {}, {}, []

    def ring_step(k):
        spot = blocks.at[block_at(1 - k)]
        ring_right[k] = copy(spot, spot, er_send.at[k], er_recv.at[k], at_z(1))
        if k < 8:
            spot = blocks.at[block_at(k - 1)]
            ring_left[k] = copy(spot, spot, el_send.at[k], el_recv.at[k], at_z(15))

    def swap(d):
        spot = blocks.at[block_at(d)]
        swaps.append(copy(spot, spot, ec_send.at[d % 16], ec_recv.at[d % 16], partner))

    def advance(k):
        ring_right[k].wait_recv()
        if k < 8:
            ring_left[k].wait_recv()
            ring_step(k + 1)
            swap(k)
        swap(-k)

    for made in local:
        made.wait()
    fulls = (full_q, full_g, full_d)
    for full, g, e in zip(fulls, (qg, gg, dg), (qe, ge, de)):
        full[...] = g[0].astype(f32) + e[0]
    starts = (0, cols[0], cols[0] + cols[1])
    spans = ((0, rows[0]), (rows[0], rows[0] + rows[1]), (0, rows[2]))
    for m, b in enumerate((qb, gb, db)):
        basis[:, starts[m] : starts[m] + cols[m]] = b[...]
    lands = (land_q, land_g, land_d, land_v)
    for land, w, m in zip(lands, (qw, gw, dw), (qm, gm, dm)):
        land[y] = w[0, 0] - (step_size * momentum_decay) * m[0, 0]
    land_v[y] = jnp.zeros((8, 128), f32)
    land_v[y, 0:1, : vec.shape[1]] = vec[...].astype(f32)
    early = []

    def send_early():
        for k, land in enumerate(lands):
            for d in (1, 2, 3):
                early.append(copy(land.at[y], land.at[y], u_send.at[k, d], u_recv.at[k, d], at_y(d)))

    def gather_ids():
        finish(swaps)
        for b in range(32):
            pair = blocks[b, per : per + 16, :].astype(f32)[0:1, :]
            id_rows[b // 4, :, (b % 4) * per : (b % 4 + 1) * per] = pair[:, :per] + 256.0 * pair[:, per:]

    def sum_rows(d, target):
        owner = (y + d) % 4
        spots = lax.broadcasted_iota(jnp.int32, (256, 4 * per), 0) + (s * 4 + owner) * block_rows
        spots = spots.astype(f32)

        def group(g, carry):
            one_hot = jnp.where(spots == id_rows[g], 1.0, 0.0).astype(jnp.bfloat16)
            values = blocks[pl.ds(4 * g, 4), :per, :].reshape(4 * per, 2 * per)
            target[...] += jnp.dot(one_hot, values, preferred_element_type=f32)
            return carry

        target[...] = jnp.zeros(target.shape, f32)
        lax.fori_loop(0, 8, group, 0)

    halves, parts, embs, tails = [], [], [], []

    def send_halves():
        halves.append(copy(part_send.at[1, pl.ds(0, 128)], part_mid.at[0], h_send.at[0], h_recv.at[0], at_y(1)))
        halves.append(copy(part_send.at[1, pl.ds(128, 128)], part_mid.at[1], h_send.at[1], h_recv.at[1], at_y(3)))

    def send_parts():
        finish(halves)
        part_send[0, :128] += part_mid[0]
        part_send[2, 128:] += part_mid[1]
        parts.append(copy(part_send.at[0], part_land.at[0], p_send.at[0], p_recv.at[0], at_y(1)))
        parts.append(copy(part_send.at[2], part_land.at[1], p_send.at[1], p_recv.at[1], at_y(3)))

    def update_rows():
        finish(parts)
        total = part_own[...] + (part_land[0] + part_land[1])
        moment = momentum_decay * em[...].reshape(block_rows, 2 * per) + total[:block_rows] * 0.25
        emb_moment_out[...] = moment
        emb_land[y, :block_rows] = ew[...].reshape(block_rows, 2 * per) - step_size * moment
        emb_land[y, block_rows:] = jnp.zeros((256 - block_rows, 2 * per), f32)
        embs.append(copy(emb_land.at[y], emb_land.at[y], e_send.at[0], e_recv.at[0], at_y(1)))
        embs.append(copy(emb_land.at[y], emb_land.at[y], e_send.at[1], e_recv.at[1], at_y(3)))

    def forward_rows():
        finish(embs)
        spot = emb_land.at[(y + 3) % 4, pl.ds(0, 128)]
        tails.append(copy(spot, spot, f_send.at[0], f_recv.at[0], at_y(1)))
        spot = emb_land.at[(y + 1) % 4, pl.ds(128, 128)]
        tails.append(copy(spot, spot, f_send.at[1], f_recv.at[1], at_y(3)))

    def first_ids():
        gather_ids()
        sum_rows(2, part_send.at[1])

    def ring_and_early():
        advance(5)
        send_early()

    def parts_and_own():
        send_parts()
        sum_rows(0, part_own)

    beside = {(0, k): (lambda k=k: advance(k + 1)) for k in range(8)}
    beside[0, 4] = ring_and_early
    beside[1, 0] = first_ids
    beside[1, 1] = lambda: sum_rows(1, part_send.at[0])
    beside[1, 2] = send_halves
    beside[1, 3] = lambda: sum_rows(3, part_send.at[2])
    beside[1, 4] = parts_and_own
    beside[1, 5] = update_rows
    beside[1, 6] = forward_rows

    def phase(r, k, copies):
        if (r, k) in beside:
            beside[r, k]()
        finish(copies)

    for r in range(ROUNDS):
        for m in range(3):
            part = dot_nt(basis[:, starts[m] : starts[m] + cols[m]], fulls[m][...])
            xbuf[r, x, m // 2, :, spans[m][0] : spans[m][1]] = part
        if r == 0:
            pl.semaphore_wait(barrier, len(peers))
            ring_step(1)
            swap(0)
        phase(r, 0, [copy(xbuf.at[r, x], xbuf.at[r, x], x_send.at[r, d], x_recv.at[r, d], at_x(d)) for d in (1, 2, 3)])
        ybuf[r, y] = (xbuf[r, 0] + xbuf[r, 1]) + (xbuf[r, 2] + xbuf[r, 3])
        phase(r, 1, [copy(ybuf.at[r, y], ybuf.at[r, y], y_send.at[r, d], y_recv.at[r, d], at_y(d)) for d in (1, 2, 3)])
        both = (ybuf[r, 0] + ybuf[r, 1]) + (ybuf[r, 2] + ybuf[r, 3])
        left = [both[m // 2][:, spans[m][0] : spans[m][1]] for m in range(3)]
        for m in range(3):
            raw = dot_nn(left[m], fulls[m][...])
            for c in range(cols[m] // 128):
                chunk = starts[m] // 128 + c
                wide[r, :, chunk // HALF * 16 + chunk % HALF] = raw[:, c * 128 : (c + 1) * 128].reshape(4, 8, 128)
            gram = dot_nt(left[m], left[m]) * 0.25
            wide[r, :, HALF + m, :, :RANK] = gram.reshape(4, 8, RANK)
            wide[r, :, 16 + HALF + m, :, :RANK] = gram.reshape(4, 8, RANK)
        phase(r, 2, [
            copy(wide.at[r, :, pl.ds(other * 16, USED)], from_core.at[r], c_send.at[r], c_recv.at[r], partner)
        ])
        half[r] = wide[r, :, pl.ds(core * 16, USED)] + from_core[r]
        phase(r, 3, [
            copy(half.at[r, (y + d) % 4], from_y.at[r, d - 1], ry_send.at[r, d], ry_recv.at[r, d], at_y(d))
            for d in (1, 2, 3)
        ])
        mine[r, :USED] = (half[r, y] + from_y[r, 0]) + (from_y[r, 1] + from_y[r, 2])
        phase(r, 4, [
            copy(mine.at[r, (z + d) % 16], from_z.at[r, d - 1], rz_send.at[r, d], rz_recv.at[r, d], at_z(d))
            for d in range(1, 16)
        ])
        tiles = [mine[r, z]] + [from_z[r, k] for k in range(15)]
        while len(tiles) > 1:
            tiles = [tiles[k] + tiles[k + 1] for k in range(0, len(tiles), 2)]
        whole[r, core, y, z] = tiles[0]
        spot = whole.at[r, core, y, z]
        phase(r, 5, [copy(spot, spot, gz_send.at[r, d], gz_recv.at[r, d], at_z(d)) for d in range(1, 16)])
        spot_y = whole.at[r, core, y, pl.ds(0, USED)]
        phase(r, 6, [copy(spot_y, spot_y, gy_send.at[r, d], gy_recv.at[r, d], at_y(d)) for d in (1, 2, 3)])
        spot_c = whole.at[r, core, :, pl.ds(0, USED)]
        last = copy(spot_c, spot_c, gc_send.at[r], gc_recv.at[r], partner)
        if (r, 7) in beside:
            beside[r, 7]()
        inverses = inverse_factors([whole[r, core, :, HALF + m].reshape(RANK, 128) for m in range(3)])
        if r == ROUNDS - 1:
            orthos = [dot_nn(inverses[m], left[m]).T for m in range(3)]
        finish([last])
        for m in range(3):
            first = starts[m] // 128
            chunks = [
                whole[r, c // HALF, :, c % HALF].reshape(RANK, 128) for c in range(first, first + cols[m] // 128)
            ]
            basis[:, starts[m] : starts[m] + cols[m]] = dot_nn(inverses[m], jnp.concatenate(chunks, axis=1))
    finish(early)
    outs = ((new_q, err_q, mom_q, qm), (new_g, err_g, mom_g, gm), (new_d, err_d, mom_d, dm))
    for m, (new, err, mom, old) in enumerate(outs):
        approx = dot_nn(orthos[m], basis[:, starts[m] : starts[m] + cols[m]]) * 0.25
        err[0] = fulls[m][...] - approx
        new[...] = approx
        own = old.shape[2]
        mom[0, 0] = momentum_decay * old[0, 0] + new[pl.ds(pl.multiple_of(y * own, own), own), :]
        new[...] = lands[m][...].reshape(rows[m], cols[m]) - step_size * approx
    vec_sum[...] = (land_v[0] + land_v[1]) + (land_v[2] + land_v[3])
    for made in list(ring_right.values()) + list(ring_left.values()):
        made.wait_send()
    finish(tails)
    for k in range(4):
        emb_out[k * block_rows : (k + 1) * block_rows, :] = emb_land[k, :block_rows]


def power_sgd(matrices, emb_grad, emb_weight, emb_moment, emb_ids, vec_tile):
    rows = tuple(matrix[0].shape[1] for matrix in matrices)
    cols = tuple(matrix[0].shape[2] for matrix in matrices)
    block_rows, _, width = emb_weight.shape
    per = emb_ids.shape[1]
    far = [operand for matrix in matrices for operand in matrix] + [emb_grad, emb_weight, emb_moment]
    f32 = jnp.float32
    shards = [matrix[3].shape[2:] for matrix in matrices]
    out_shape = [jax.ShapeDtypeStruct((rows[m], cols[m]), f32) for m in range(3)]
    out_shape += [jax.ShapeDtypeStruct((1, rows[m], cols[m]), f32) for m in range(3)]
    out_shape += [jax.ShapeDtypeStruct((1, 1) + shape, f32) for shape in shards]
    out_shape += [jax.ShapeDtypeStruct((8, 128), f32)]
    out_shape += [jax.ShapeDtypeStruct((4 * block_rows, width), f32), jax.ShapeDtypeStruct((block_rows, width), f32)]
    dma = pltpu.SemaphoreType.DMA
    scratch = [pltpu.VMEM(operand.shape, operand.dtype) for matrix in matrices for operand in matrix]
    scratch += [pltpu.VMEM((block_rows, 1, width), f32)] * 2
    scratch += [pltpu.VMEM((rows[m], cols[m]), f32) for m in range(3)]
    scratch += [pltpu.VMEM((RANK, sum(cols)), f32)]
    scratch += [pltpu.VMEM((4,) + shape, f32) for shape in shards]
    scratch += [
        pltpu.VMEM((4, 8, 128), f32),
        pltpu.VMEM((ROUNDS, 4, 2, RANK, 128), f32),
        pltpu.VMEM((ROUNDS, 4, 2, RANK, 128), f32),
        pltpu.VMEM((ROUNDS, 4, 32, 8, 128), f32),
        pltpu.VMEM((ROUNDS, 4, USED, 8, 128), f32),
        pltpu.VMEM((ROUNDS, 4, USED, 8, 128), f32),
        pltpu.VMEM((ROUNDS, 3, USED, 8, 128), f32),
        pltpu.VMEM((ROUNDS, 16, 8, 128), f32),
        pltpu.VMEM((ROUNDS, 15, 8, 128), f32),
        pltpu.VMEM((ROUNDS, 2, 4, 16, 8, 128), f32),
        pltpu.VMEM((32, per + 16, width), jnp.bfloat16),
        pltpu.VMEM((8, 1, 4 * per), f32),
        pltpu.VMEM((256, width), f32),
        pltpu.VMEM((3, 256, width), f32),
        pltpu.VMEM((2, 128, width), f32),
        pltpu.VMEM((2, 256, width), f32),
        pltpu.VMEM((4, 256, width), f32),
        dma((18,)),
    ]
    for shape in (
        (4, 4), (ROUNDS, 4), (ROUNDS, 4), (ROUNDS,), (ROUNDS, 4), (ROUNDS, 16), (ROUNDS, 16), (ROUNDS, 4), (ROUNDS,),
        (9,), (9,), (16,), (2,), (2,), (2,), (2,),
    ):
        scratch += [dma(shape), dma(shape)]
    vmem = pl.BlockSpec(memory_space=pltpu.VMEM)

    def body(*refs):
        sgd_kernel(rows, cols, block_rows, *refs)

    return pl.pallas_call(
        body,
        out_shape=out_shape,
        in_specs=[pl.BlockSpec(memory_space=pl.ANY)] * len(far) + [vmem] * 2,
        out_specs=[vmem] * len(out_shape),
        scratch_shapes=scratch,
        compiler_params=pltpu.CompilerParams(collective_id=0, has_side_effects=True),
        name="power_sgd",
    )(*far, emb_ids, vec_tile)


def place(arrays):
    count = len(arrays)

    def body(*refs):
        sources, targets = refs[:count], refs[count : 2 * count]
        held, load, store = refs[2 * count : 3 * count], refs[3 * count], refs[3 * count + 1]
        loads = [pltpu.make_async_copy(sources[k], held[k], load.at[k]) for k in range(count)]
        stores = [pltpu.make_async_copy(held[k], targets[k], store.at[k]) for k in range(count)]
        for made in loads:
            made.start()
        for k in range(count):
            loads[k].wait()
            stores[k].start()
        for made in stores:
            made.wait()

    far = pl.BlockSpec(memory_space=pl.ANY)
    return pl.pallas_call(
        body,
        out_shape=[jax.ShapeDtypeStruct(a.shape, a.dtype) for a in arrays],
        in_specs=[far] * count,
        out_specs=[far] * count,
        scratch_shapes=[pltpu.VMEM(a.shape, a.dtype) for a in arrays] + [pltpu.SemaphoreType.DMA((count,))] * 2,
        name="place",
    )(*arrays)


def on_device(
    qkv_grad, qkv_error, qkv_basis, qkv_weight, qkv_moment,
    gu_grad, gu_error, gu_basis, gu_weight, gu_moment,
    down_grad, down_error, down_basis, down_weight, down_moment,
    vec_grad, vec_weight, vec_moment,
    emb_ids, emb_grad, emb_weight, emb_moment,
):
    rep_count = lax.axis_size("rep")
    vec_len = vec_weight.shape[0]
    block_rows, width = emb_weight.shape[2:]
    outs = power_sgd(
        (
            (qkv_grad, qkv_error, qkv_basis.T, qkv_weight, qkv_moment),
            (gu_grad, gu_error, gu_basis.T, gu_weight, gu_moment),
            (down_grad, down_error, down_basis.T, down_weight, down_moment),
        ),
        emb_grad, emb_weight.reshape(block_rows, 1, width), emb_moment.reshape(block_rows, 1, width), emb_ids, vec_grad,
    )
    vec_sum, emb_moment_new = outs[9], outs[11]
    new_q, new_g, new_d, err_q, err_g, err_d, mom_q, mom_g, mom_d, emb_new = place(list(outs[:9]) + [outs[10]])
    vec_mean = vec_sum[0, :vec_len] / rep_count
    vec_moment_new = momentum_decay * vec_moment + vec_mean
    vec_new = vec_weight - step_size * vec_moment_new
    return (
        new_q, err_q, mom_q, new_g, err_g, mom_g, new_d, err_d, mom_d,
        vec_new, vec_moment_new, emb_new, emb_moment_new[None, None],
    )


def solution(mesh):
    grouped = P("shard", "rep", None, "tp")
    matrix = P("rep", "shard", "tp")
    per_matrix = (matrix, matrix, P("tp", None), grouped, grouped)
    vector = P(("shard", "tp"))
    return jax.shard_map(
        on_device,
        mesh=mesh,
        in_specs=per_matrix * 3
        + (P("rep", ("shard", "tp")), vector, vector, P("rep", "shard"), matrix, grouped, grouped),
        out_specs=(P("shard", "tp"), matrix, grouped) * 3 + (vector, vector, P("shard", "tp"), grouped),
        check_vma=False,
    )
```
